32 devices in a mesh: groups: 2 (over x), ctx: 16 (over z, y, core).
Axes of the slice: x: 2, y: 2, z: 4, core: 2. Of those that a mesh axis runs over, the one named last changes fastest.
Arguments:
- hidden_rows: bfloat16 [16384, 4096], P(('groups', 'ctx')), parts along dimension 0, may hold values from -6 to 6
- positions: int32 [16384], P(('groups', 'ctx')), parts along dimension 0, may hold values from 0 to 32767
- owners: int32 [16384, 1], P(('groups', 'ctx')), parts along dimension 0, may hold values from 0 to 15; in each aligned block of 512 rows (0 to 511, 512 to 1023, ...) at most 64 rows name the same one
- lengths: int32 [8], P('groups'), parts along dimension 0, may hold values from 1 to 4096, 8192 in all
- queries: bfloat16 [32, 8192], P(('groups', 'ctx')), parts along dimension 0, may hold values from -400 to 400
- ln_gain: float32 [4096], replicated, may hold values from 0.1 to 1.9
- w_key: bfloat16 [4096, 512], replicated, may hold values from -0.09375 to 0.09375
- w_value: bfloat16 [4096, 512], replicated, may hold values from -0.09375 to 0.09375
- k_gain: float32 [128], replicated, may hold values from 0.1 to 1.9
Outputs:
- attended: bfloat16 [32, 8192], P(('groups', 'ctx')), parts along dimension 0
- key_cache: bfloat16 [32768, 512], P(('groups', 'ctx')), parts along dimension 0
- value_cache: bfloat16 [32768, 512], P(('groups', 'ctx')), parts along dimension 0
The draws below stay inside these ranges and needn't reach their ends.
There are 2 independent parts, one for each index of `groups`. The reference program is written for one: setup_inputs(seed, part) draws one part's arguments, and reference() takes and returns one part's arrays. A program takes and returns all parts, laid end to end along the dimension named above; an argument that names none is the same for every part. Nothing has to cross between parts.
Inputs may be any that keep to these rules, and one draw needn't show every extreme that they name: `owners`: among the rows of one device at most 64 name the same shard, and in every draw some shard is named by exactly 64 rows of some device. The lengths sum to 8192; conversations follow one another in row order.
All inputs are finite; a program needn't handle non-finite values.
Results may differ from the reference program's by a relative error of at most 0.015.
The reference program's roundings to bfloat16 on the way count: a program that leaves them out, or rounds other values in their place, can miss the bound.
Values may be sent and summed in bfloat16 or wider, within the bound.
A program may use at most 128 MiB of HBM per device.

```python
import math
import jax
import jax.numpy as jnp
import numpy as np
from jax import lax

D = 4096
H = 64
KVH = 4
HD = 128
ROWS_DEV = 512
CONV = 4
ROWS = 8192
QUERIES = 16
QC = 4
CAP = 64
N_CTX = 16


def draw_queries(key, part):
    first = jax.random.fold_in(jax.random.fold_in(key, 7), 0)
    base = jnp.clip(jax.random.normal(first, (QUERIES, H * HD), jnp.float32), -6.0, 6.0)
    return base.astype(jnp.bfloat16)


def set_ends(array, key, smallest, top_value):
    dims = array.shape
    index_at = [jax.random.randint(jax.random.fold_in(key, axis), (), 0, dims[axis]) for axis in range(len(dims))]
    array = array.at[tuple(index_at)].set(smallest)
    longest = dims.index(max(dims))
    index_at[longest] = (index_at[longest] + 1) % dims[longest]
    return array.at[tuple(index_at)].set(top_value)


def shard_levels(rng, dims, pieces, smallest, high):
    gain, own = 1.0, jax.random.fold_in(rng, 6)
    for dim, parts in pieces:
        steps = jnp.exp(jax.random.uniform(jax.random.fold_in(own, dim), (parts,), jnp.float32, smallest / len(pieces), high / len(pieces)))
        gain = gain * jnp.repeat(steps, dims[dim] // parts).reshape([-1 if axis == dim else 1 for axis in range(len(dims))])
    return gain


def profile(number_of, total, limit, slope):
    loads = [(1 << 20) // math.isqrt(grade ** slope) + 1 for grade in range(2, number_of + 1)]
    surplus, holding = total - limit - (number_of - 1), [1] * (number_of - 1)
    while surplus > 0:
        candidates = [i for i in range(number_of - 1) if holding[i] < limit]
        mass, remaining = sum([loads[i] for i in candidates]), surplus
        for i in candidates:
            addition = min(limit - holding[i], max(1, remaining * loads[i] // mass), surplus)
            holding[i] = holding[i] + addition
            surplus = surplus - addition
    return np.array([limit] + holding)


def uneven(own_key, count, total, most, slope):
    if count == 2:
        one = jax.random.randint(own_key, (), max(1, total - most), min(most, total - 1) + 1)
        return jnp.stack([one, total - one])
    tallies = jnp.asarray(profile(count, total, most, slope), jnp.int32)
    twos = (count - 1) // 2
    source_of, taker = tallies[1:1 + 2 * twos:2], tallies[2:2 + 2 * twos:2]
    margin = jnp.minimum(source_of - 1, most - taker)
    shifted = jax.random.randint(jax.random.fold_in(own_key, 1), (twos,), 0, 1 << 20) % (margin + 1)
    tallies = tallies.at[1:1 + 2 * twos:2].set(source_of - shifted).at[2:2 + 2 * twos:2].set(taker + shifted)
    return tallies[jax.random.permutation(jax.random.fold_in(own_key, 2), count)]


def shared_out(key, own, number, rows, count, top, most, skew):
    order = jax.random.permutation(key, count)
    heavy_load, common = shares(count, rows * top, most, skew, True), shares(count, rows * top, most, skew, False)
    places = jnp.arange(count)

    def named(sizes, turn):
        used = int((sizes > 0).sum())
        fixed = max(1, used // 4)
        shifted = fixed + (places - fixed + turn * (used - fixed)) % max(1, count - fixed)
        return jnp.zeros((count,), jnp.int32).at[order[jnp.where(places < fixed, places, shifted)]].set(jnp.asarray(sizes, jnp.int32))

    sizes = jnp.where(number % 4 == 0, named(heavy_load, number // 4), named(common, number - number // 4 - 1))
    mixed = jax.random.permutation(jax.random.fold_in(own, 3), count)
    giver, sink = mixed[0:count // 2 * 2:2], mixed[1:count // 2 * 2:2]
    margin = jnp.minimum(sizes[giver] - 1, most - sizes[sink]) // 2
    margin = jnp.where((giver == order[0]) | (sink == order[0]) | (sizes[sink] == 0), 0, jnp.maximum(margin, 0))
    shifted = jax.random.randint(jax.random.fold_in(own, 4), (count // 2,), 0, 1 << 20) % (margin + 1)
    sizes = sizes.at[giver].add(-shifted).at[sink].add(shifted)
    members = jnp.searchsorted(jnp.cumsum(sizes), jnp.arange(rows * top), side="right").astype(jnp.int32)
    grid = members.reshape(top, rows).T
    grid = grid[jax.random.permutation(jax.random.fold_in(own, 1), rows)]
    turn = jax.random.randint(jax.random.fold_in(own, 2), (rows, 1), 0, top)
    return jnp.take_along_axis(grid, (jnp.arange(top)[None, :] + turn) % top, axis=1)


def shares(number_of, total, limit, lean, full):
    weights = [(1 << 20) // math.isqrt(grade ** lean) + 1 for grade in range(1, number_of + 1)]
    largest = limit if full else min(limit, max(-(-total // number_of), total * weights[0] // sum(weights)))
    least = 1 if total - largest >= number_of - 1 else 0
    holding, spare = [largest] + [least] * (number_of - 1), total - largest - least * (number_of - 1)
    while spare > 0:
        movable = [i for i in range(1, number_of) if holding[i] < largest] or [i for i in range(1, number_of) if holding[i] < limit]
        whole, remaining = sum([weights[i] for i in movable]), spare
        for i in movable:
            extra = min(limit - holding[i], max(1, remaining * weights[i] // whole), spare)
            holding[i] = holding[i] + extra
            spare = spare - extra
    return np.array(holding)


def bell_draw(rng, extent, width, limit, cuts=(), held_as=jnp.bfloat16):
    array = width * jax.random.normal(rng, extent, jnp.float32)
    if cuts:
        array = array * shard_levels(rng, extent, cuts, -0.22, 0.18)
    return jnp.clip(array, -limit, limit).astype(held_as)


def setup_inputs(seed: int = 0, part: int = 0) -> dict:
    streams_of = jax.random.split(jax.random.key(seed), 10)
    part_keys = jax.random.split(jax.random.fold_in(streams_of[9], part), 10)
    hidden_rows = bell_draw(part_keys[0], (ROWS, D), 1.0, 6.0, ((0, 16),))
    positions = set_ends(jax.random.randint(part_keys[1], (ROWS,), 0, 32768), jax.random.fold_in(part_keys[1], 1), 0, 32767).astype(jnp.int32)
    owners_keys = jax.random.split(jax.random.fold_in(part_keys[2], 1), ROWS // ROWS_DEV)
    owners_turns = jax.random.permutation(jax.random.fold_in(part_keys[2], 3), ROWS // ROWS_DEV)
    owners = jax.vmap(lambda own, number: shared_out(jax.random.fold_in(part_keys[2], 2), own, number, ROWS_DEV, N_CTX, 1, CAP, 2))(owners_keys, owners_turns).reshape((ROWS, 1))
    lengths = uneven(part_keys[3], CONV, ROWS, ROWS // 2, 2).astype(jnp.int32)
    queries = draw_queries(jax.random.fold_in(jax.random.fold_in(streams_of[9], part), 71), part)
    ln_gain = jnp.clip(1.0 + 0.18 * jax.random.normal(streams_of[5], (D,), jnp.float32), 0.1, 1.9)
    w_key = bell_draw(streams_of[6], (D, KVH * HD), D ** -0.5, 0.09375)
    w_value = bell_draw(streams_of[7], (D, KVH * HD), D ** -0.5, 0.09375)
    k_gain = jnp.clip(1.0 + 0.18 * jax.random.normal(streams_of[8], (HD,), jnp.float32), 0.1, 1.9)
    return {"hidden_rows": hidden_rows, "positions": positions, "owners": owners, "lengths": lengths, "queries": queries, "ln_gain": ln_gain, "w_key": w_key, "w_value": w_value, "k_gain": k_gain}


EPSILON = 1e-06
THETA = 1000000.0

def rotate(key_heads, places):
    half = key_heads.shape[-1] // 2
    freqs = THETA ** (-(jnp.arange(half, dtype=jnp.float32) * 2.0) / key_heads.shape[-1])
    angles = places.astype(jnp.float32)[:, None] * freqs[None, :]
    cosine = jnp.concatenate([jnp.cos(angles), jnp.cos(angles)], axis=-1)[:, None, :]
    sine = jnp.concatenate([jnp.sin(angles), jnp.sin(angles)], axis=-1)[:, None, :]
    turned = jnp.concatenate([-key_heads[..., half:], key_heads[..., :half]], axis=-1)
    return key_heads * cosine + turned * sine

def restore(rows, places, ln_gain, w_key, w_value, k_gain):
    wide = rows.astype(jnp.float32)
    normed = (wide * lax.rsqrt(lax.optimization_barrier(jnp.mean(wide * wide, axis=-1, keepdims=True)) + EPSILON) * ln_gain).astype(jnp.bfloat16)
    raw_keys = jnp.dot(normed, w_key, preferred_element_type=jnp.float32)
    key_heads = raw_keys.reshape(rows.shape[0], -1, k_gain.shape[0])
    key_heads = key_heads * lax.rsqrt(lax.optimization_barrier(jnp.mean(key_heads * key_heads, axis=-1, keepdims=True)) + EPSILON) * k_gain
    key_rows = rotate(key_heads, places).reshape(rows.shape[0], -1).astype(jnp.bfloat16)
    value_rows = jnp.dot(normed, w_value, preferred_element_type=jnp.float32).astype(jnp.bfloat16)
    return (key_rows, value_rows)

def reference(hidden_rows, positions, owners, lengths, queries, ln_gain, w_key, w_value, k_gain):
    key_rows, value_rows = restore(hidden_rows, positions, ln_gain, w_key, w_value, k_gain)
    ends = jnp.cumsum(lengths)
    row_index = jnp.arange(ROWS, dtype=jnp.int32)
    row_conv = lax.optimization_barrier(jnp.sum((row_index[:, None] >= ends[None, :]).astype(jnp.int32), axis=1))
    query_conv = jnp.arange(QUERIES, dtype=jnp.int32) // QC
    group = H // KVH
    keys3 = key_rows.reshape(ROWS, KVH, HD).astype(jnp.float32)
    values3 = value_rows.reshape(ROWS, KVH, HD).astype(jnp.float32)
    block = 8

    def one_block(index):
        start = (index * block).astype(jnp.int32)
        query_block = lax.dynamic_slice_in_dim(queries, start, block, 0).astype(jnp.float32).reshape(block, KVH, group, HD)
        conv_block = lax.dynamic_slice_in_dim(query_conv, start, block, 0)
        scores = jnp.einsum('qkgd,skd->qkgs', query_block, keys3) / jnp.sqrt(jnp.float32(HD))
        allowed = (conv_block[:, None] == row_conv[None, :])[:, None, None, :]
        scores = jnp.where(allowed, scores, -1e+30)
        peak = lax.optimization_barrier(jnp.max(scores, axis=-1, keepdims=True))
        expos = jnp.where(allowed, jnp.exp(scores - peak), 0.0)
        totals = lax.optimization_barrier(jnp.sum(expos, axis=-1))
        rounded = expos.astype(jnp.bfloat16).astype(jnp.float32)
        mixed = jnp.einsum('qkgs,skd->qkgd', rounded, values3) / totals[..., None]
        return mixed.reshape(block, H * HD)
    attended = lax.map(one_block, jnp.arange(QUERIES // block, dtype=jnp.int32)).reshape(QUERIES, H * HD).astype(jnp.bfloat16)
    target = owners[:, 0].reshape(N_CTX, ROWS_DEV)
    onehot = (target[:, :, None] == jnp.arange(N_CTX, dtype=jnp.int32)[None, None, :]).astype(jnp.int32)
    ranks = lax.optimization_barrier(jnp.sum((jnp.cumsum(onehot, axis=1) - onehot) * onehot, axis=-1))
    slot = target * (N_CTX * CAP) + jnp.arange(N_CTX, dtype=jnp.int32)[:, None] * CAP + ranks
    slot = slot.reshape(-1).astype(jnp.int32)
    key_cache = jnp.zeros((N_CTX * N_CTX * CAP, KVH * HD), jnp.bfloat16).at[slot].set(key_rows)
    value_cache = jnp.zeros((N_CTX * N_CTX * CAP, KVH * HD), jnp.bfloat16).at[slot].set(value_rows)
    return (attended, key_cache, value_cache)
```

```python
import functools

import jax
import jax.numpy as jnp
import numpy as np
from jax import lax
from jax.experimental import pallas as pl
from jax.experimental.pallas import tpu as pltpu
from jax.sharding import PartitionSpec as P

EPSILON = 1e-06
THETA = 1000000.0
MASKED = -1e30
MESH = pl.DeviceIdType.MESH
F32 = jnp.float32
BF16 = jnp.bfloat16


def xor(a, b, n):
    out, bit = 0, 1
    while bit < n:
        p, q = (a // bit) % 2, (b // bit) % 2
        out = out + bit * (p + q - 2 * p * q)
        bit *= 2
    return out


def fast_kernel(n, plane, cap, hd, fill, x_ref, wk_ref, wv_ref, len_in, own_in, pos_in, freq_in, q_in, gain_in, kg_in,
                att_ref, key_ref, val_ref, over_ref,
                x, w, normed, kv, onehot, pick, pack, far, gate, place, ward, flat, mine, q_all, part, stat, pa, sa,
                mid_p, mid_s, pb, sb, turn, goes, comes, over, overs,
                len_ref, own_ref, pos_ref, freq_ref, q_ref, gain_ref, kg_ref,
                small_sem, x_sem, w_sem, own_sem, kv_send, kv_recv, hop_send, hop_recv,
                far_send, gate_recv, ward_send, ward_recv, note_send, note_recv):
    me = lax.axis_index("ctx")
    grp = lax.axis_index("groups")
    grps = lax.axis_size("groups")
    lines = n // plane
    line, spot = me // plane, me % plane
    half = n // 2
    deep = lines // 2
    side = me // half
    near = side * half
    gate_line = side * (deep - 1) + (1 - side) * deep
    my_gate = gate_line * plane + spot
    is_gate = line == (1 - side) * (deep - 1) + side * deep
    rows, width = x.shape
    heads = mine.shape[0]
    kvh = wk_ref.shape[1] // hd
    group = heads // kvh
    chunk = w.shape[2]
    per = wk_ref.shape[1] // chunk
    chunks = 2 * per
    hopped = gate.shape[0]

    def loop(count, body):
        def step(i, carry):
            body(i)
            return carry
        lax.fori_loop(1, count, step, 0)

    def every(body):
        loop(n, lambda i: body(xor(me, n - i, n)))

    def beside(body):
        loop(half, lambda i: body(xor(me, half - i, n)))

    def others(body):
        loop(grps, lambda i: body((grp + i) % grps, i - 1))

    barrier = pltpu.get_barrier_semaphore()
    every(lambda d: pl.semaphore_signal(barrier, inc=1, device_id=(grp, d), device_id_type=MESH))
    others(lambda g, i: pl.semaphore_signal(barrier, inc=1, device_id=(g, me), device_id_type=MESH))

    smalls = {}
    for i, (name, src, dst) in enumerate((
        ("q", q_in, q_ref), ("own", own_in, own_ref), ("gain", gain_in, gain_ref), ("len", len_in, len_ref),
        ("pos", pos_in, pos_ref), ("freq", freq_in, freq_ref), ("kg", kg_in, kg_ref),
    )):
        smalls[name] = pltpu.make_async_copy(src, dst, small_sem.at[i])
        smalls[name].start()
    x_parts = x_sem.shape[0]
    xr = rows // x_parts
    x_copies = [
        pltpu.make_async_copy(x_ref.at[pl.ds(i * xr, xr)], x.at[pl.ds(i * xr, xr)], x_sem.at[i])
        for i in range(x_parts)
    ]
    for copy in x_copies:
        copy.start()
    w_copies = []
    for c in range(chunks):
        src = wv_ref if c < per else wk_ref
        copy = pltpu.make_async_copy(src.at[:, pl.ds((c % per) * chunk, chunk)], w.at[c], w_sem.at[c])
        w_copies.append(copy)
    w_copies[0].start()

    smalls["q"].wait()
    for h in range(heads):
        flat[h:h + 1, :] = q_ref[:, h * hd:(h + 1) * hd].astype(F32)
    mine[...] = flat[...].astype(BF16)

    smalls["own"].wait()
    own = own_ref[...]
    named = jnp.where(lax.broadcasted_iota(jnp.int32, (n, rows), 0) == own, 1.0, 0.0)
    afar = jnp.where(own // half == side, 0.0, 1.0)
    marks = jnp.concatenate([named, jnp.broadcast_to(afar, (16, rows))], axis=0)
    earlier = jnp.where(
        lax.broadcasted_iota(jnp.int32, (rows, rows), 0) < lax.broadcasted_iota(jnp.int32, (rows, rows), 1), 1.0, 0.0
    ).astype(BF16)
    before = jnp.dot(marks.astype(BF16), earlier, preferred_element_type=F32)
    rank = jnp.sum(before[:n] * named, axis=0, keepdims=True)
    slot = own.astype(F32) * cap + rank
    slots = n * cap
    step = 128
    for b in range(slots // step):
        places = (lax.broadcasted_iota(jnp.int32, (step, rows), 0) + b * step).astype(F32)
        onehot[pl.ds(b * step, step), :] = jnp.where(places == slot, 1.0, 0.0).astype(BF16)
    seat = jnp.where(afar > 0.0, before[n:n + 1], -1.0)
    for b in range(fill // step):
        places = (lax.broadcasted_iota(jnp.int32, (step, rows), 0) + b * step).astype(F32)
        pick[pl.ds(b * step, step), :] = jnp.where(places == seat, 1.0, 0.0).astype(BF16)
    there = own.astype(F32) + 1.0
    facts = jnp.where(lax.broadcasted_iota(jnp.int32, (16, rows), 0) == 0, there, rank).astype(BF16)
    told = lax.dot_general(facts, pick[...], (((1,), (1,)), ((), ())), preferred_element_type=F32)
    goes[...] = (told[0:1] - 1.0 - ((1 - side) * half).astype(F32)) * cap + told[1:2]
    full = jnp.where(jnp.sum(afar, axis=1, keepdims=True) > fill, 1.0, 0.0)
    over[...] = jnp.broadcast_to(full, over.shape)

    def send(src, dst, s_sem, r_sem, d):
        pltpu.make_async_remote_copy(
            src_ref=src, dst_ref=dst, send_sem=s_sem, recv_sem=r_sem, device_id=(grp, d), device_id_type=MESH
        ).start()

    def tell(g, i):
        pltpu.make_async_remote_copy(
            src_ref=over, dst_ref=overs.at[i], send_sem=note_send.at[1], recv_sem=note_recv.at[1],
            device_id=(g, me), device_id_type=MESH
        ).start()

    def whole(ref, sem):
        pltpu.make_async_copy(ref, ref, sem).wait()

    def on_line(body):
        loop(lines, lambda i: body(xor(line, lines - i, lines)))

    def on_plane(body):
        loop(plane, lambda i: body(xor(spot, plane - i, plane)))

    smalls["gain"].wait()
    gain = gain_ref[...]
    tile = 16
    for i in range(x_parts):
        x_copies[i].wait()

        def norm(t, carry):
            at = pl.ds(pl.multiple_of(i * xr + t * tile, tile), tile)
            wide = x[at, :].astype(F32)
            scale = lax.rsqrt(jnp.mean(wide * wide, axis=-1, keepdims=True) + EPSILON)
            normed[at, :] = (wide * scale * gain).astype(BF16)
            return carry
        lax.fori_loop(0, xr // tile, norm, 0, unroll=True)
        if i == 0:
            for copy in w_copies[1:]:
                copy.start()

    own_copies = []

    def target(c):
        return val_ref if c < per else key_ref, pl.ds((c % per) * chunk, chunk)

    def keep(c):
        out_ref, cols = target(c)
        copy = pltpu.make_async_copy(pack.at[c, me], out_ref.at[me, :, cols], own_sem.at[c])
        copy.start()
        own_copies.append(copy)

    def hop(c):
        out_ref, cols = target(c)
        far[c] = jnp.dot(pick[...], kv[c], preferred_element_type=F32).astype(BF16)
        send(far.at[c], gate.at[c, line % deep], far_send.at[c], gate_recv.at[c], my_gate)
        at = pl.ds(pl.multiple_of(near * cap, half * cap), half * cap)
        packed = jnp.dot(onehot[at, :], kv[c], preferred_element_type=F32)
        pack[c, pl.ds(near, half)] = packed.reshape(half, cap, chunk).astype(BF16)
        beside(lambda d: send(pack.at[c, d], out_ref.at[me, :, cols], kv_send.at[c], kv_recv.at[c], d))
        keep(c)

    def ship(c):
        out_ref, cols = target(c)
        packed = jnp.dot(onehot[...], kv[c], preferred_element_type=F32)
        pack[c] = packed.reshape(n, cap, chunk).astype(BF16)
        every(lambda d: send(pack.at[c, d], out_ref.at[me, :, cols], kv_send.at[c], kv_recv.at[c], d))
        keep(c)

    def forward(c):
        out_ref, cols = target(c)

        @pl.when(is_gate)
        def _():
            whole(gate.at[c], gate_recv.at[c])
            if c == 0:
                whole(comes, note_recv.at[0])
                for j in range(deep):
                    for b in range(half * cap // step):
                        places = (lax.broadcasted_iota(jnp.int32, (step, fill), 0) + b * step).astype(F32)
                        place[j, pl.ds(b * step, step), :] = jnp.where(places == comes[j], 1.0, 0.0).astype(BF16)
            for j in range(deep):
                source = ((1 - side) * deep + j) * plane + spot
                spread = jnp.dot(place[j], gate[c, j], preferred_element_type=F32)
                ward[c, j] = spread.reshape(half, cap, chunk).astype(BF16)
                beside(lambda d: send(
                    ward.at[c, j, d - near], out_ref.at[source, :, cols], ward_send.at[c], ward_recv.at[c], d))
                out_ref[source, :, cols] = ward[c, j, me - near]

    def project(c):
        w_copies[c].wait()
        raw = jnp.dot(normed[...], w[c], preferred_element_type=F32)
        if c < per:
            kv[c] = raw.astype(BF16)
            return
        for h in range(chunk // hd):
            head = raw[:, h * hd:(h + 1) * hd]
            head = head * lax.rsqrt(jnp.mean(head * head, axis=-1, keepdims=True) + EPSILON) * kg_ref[...]
            turned = pltpu.roll(head, hd // 2, 1)
            kv[c, :, h * hd:(h + 1) * hd] = (head * turn[0] + turned * turn[1]).astype(BF16)

    project(0)
    pl.semaphore_wait(barrier, n - 1 + grps - 1)
    on_line(lambda j: send(mine, q_all.at[line, spot], hop_send.at[0], hop_recv.at[0], j * plane + spot))
    send(goes, comes.at[line % deep], note_send.at[0], note_recv.at[0], my_gate)
    others(tell)
    q_all[line, spot] = mine[...]
    hop(0)
    for c in range(1, per):
        project(c)
        hop(c)
    whole(q_all.at[pl.ds(0, lines - 1), 0], hop_recv.at[0])
    on_plane(
        lambda j: send(q_all.at[:, spot], q_all.at[:, spot], hop_send.at[1], hop_recv.at[1], line * plane + j)
    )

    for name in ("len", "pos", "freq", "kg"):
        smalls[name].wait()
    angles = freq_ref[...] * pos_ref[...].astype(F32)
    cosine, sine = jnp.cos(angles), jnp.sin(angles)
    turn[0] = jnp.concatenate([cosine, cosine], axis=0).T
    turn[1] = jnp.concatenate([-sine, sine], axis=0).T
    for c in range(per, chunks):
        project(c)
        if c < hopped:
            hop(c)

    row = me * rows + lax.broadcasted_iota(jnp.int32, (1, rows), 1)
    convs = len_ref.shape[0]
    row_conv, end = jnp.zeros((1, rows), jnp.int32), 0
    for j in range(convs):
        end = end + len_ref[j]
        row_conv = row_conv + jnp.where(row >= end, 1, 0)

    whole(overs, note_recv.at[1])
    flag = over[0:1, :]
    for i in range(overs.shape[0]):
        flag = jnp.maximum(flag, overs[i, 0:1, :])

    whole(q_all.at[:, pl.ds(0, plane - 1)], hop_recv.at[1])
    span = min(lines, max(1, 16 // plane))
    lined = span * plane * group
    per_conv = n // convs
    scale = 1.0 / (hd ** 0.5)
    in_chunk = chunk // hd

    def attend(b, carry):
        first = b * span * plane
        at = pl.ds(b * span, span)
        asks = (first + lax.broadcasted_iota(jnp.int32, (lined, rows), 0) // group) // per_conv
        allowed = asks == row_conv
        lane = lax.broadcasted_iota(jnp.int32, (lined, 128), 1)
        logs = jnp.where(lane == 127, flag, 0.0)
        for k in range(kvh):
            q = q_all[at, :, k * group:(k + 1) * group, :].reshape(lined, hd)
            cols = slice((k % in_chunk) * hd, (k % in_chunk + 1) * hd)
            keys = kv[per + k // in_chunk, :, cols]
            values = kv[k // in_chunk, :, cols]
            scores = lax.dot_general(q, keys, (((1,), (1,)), ((), ())), preferred_element_type=F32) * scale
            scores = jnp.where(allowed, scores, MASKED)
            peak = jnp.max(scores, axis=-1, keepdims=True)
            expos = jnp.exp(scores - peak)
            sums = jnp.sum(expos, axis=-1, keepdims=True)
            mixed = jnp.dot(expos.astype(BF16), values, preferred_element_type=F32) / sums
            part[at, :, k * group:(k + 1) * group, :] = mixed.reshape(span, plane, group, hd).astype(BF16)
            logs = jnp.where(lane == k, peak + jnp.log(sums), logs)
        stat[at] = logs.reshape(span, plane, group, 128)
        return carry

    lax.fori_loop(0, lines // span, attend, 0)

    def give(j):
        send(part.at[:, j], pa.at[spot], hop_send.at[2], hop_recv.at[2], line * plane + j)
        send(stat.at[:, j], sa.at[spot], hop_send.at[3], hop_recv.at[3], line * plane + j)

    on_plane(give)
    pa[spot] = part[:, spot]
    sa[spot] = stat[:, spot]
    forward(0)

    def merge(count, p_at, s_at):
        top = lax.fori_loop(0, count, lambda s, t: jnp.maximum(t, s_at(s)), jnp.full((group, 128), MASKED, F32))

        def add(s, carry):
            below, sums = carry
            factor = jnp.exp(s_at(s) - top)
            sums = tuple(sums[k] + factor[:, k:k + 1] * p_at(s, k).astype(F32) for k in range(kvh))
            return below + factor, sums

        zeros = jnp.zeros((group, 128), F32), tuple(jnp.zeros((group, hd), F32) for _ in range(kvh))
        below, sums = lax.fori_loop(0, count, add, zeros)
        lane = lax.broadcasted_iota(jnp.int32, (group, 128), 1)
        logs = jnp.where(lane == 127, top, top + jnp.log(below))
        return [(sums[k] / below[:, k:k + 1]).astype(BF16) for k in range(kvh)], logs

    whole(pa.at[pl.ds(0, plane - 1)], hop_recv.at[2])
    whole(sa.at[pl.ds(0, plane - 1)], hop_recv.at[3])

    def halfway(l, carry):
        mixed, logs = merge(
            plane, lambda s, k: pa[s, l, k * group:(k + 1) * group, :], lambda s: sa[s, l]
        )
        for k in range(kvh):
            mid_p[l, k * group:(k + 1) * group, :] = mixed[k]
        mid_s[l] = logs
        return carry

    lax.fori_loop(0, lines, halfway, 0)

    def give_on(j):
        send(mid_p.at[j], pb.at[line], hop_send.at[4], hop_recv.at[4], j * plane + spot)
        send(mid_s.at[j], sb.at[line], hop_send.at[5], hop_recv.at[5], j * plane + spot)

    on_line(give_on)
    pb[line] = mid_p[line]
    sb[line] = mid_s[line]
    for c in range(hopped, chunks):
        ship(c)
    for c in range(1, hopped):
        forward(c)
    whole(pb.at[pl.ds(0, lines - 1)], hop_recv.at[4])
    whole(sb.at[pl.ds(0, lines - 1)], hop_recv.at[5])
    mixed, logs = merge(lines, lambda s, k: pb[s, k * group:(k + 1) * group, :], lambda s: sb[s])
    lane = lax.broadcasted_iota(jnp.int32, (group, 128), 1)
    over_ref[0] = jnp.max(jnp.where(lane == 127, logs, 0.0))
    for k in range(kvh):
        flat[k * group:(k + 1) * group, :] = mixed[k].astype(F32)
    for h in range(heads):
        att_ref[:, h * hd:(h + 1) * hd] = flat[h:h + 1, :].astype(BF16)

    whole(q_all.at[pl.ds(0, lines - 1), 0], hop_send.at[0])
    whole(q_all.at[:, pl.ds(0, plane - 1)], hop_send.at[1])
    whole(pa.at[pl.ds(0, plane - 1)], hop_send.at[2])
    whole(sa.at[pl.ds(0, plane - 1)], hop_send.at[3])
    whole(pb.at[pl.ds(0, lines - 1)], hop_send.at[4])
    whole(sb.at[pl.ds(0, lines - 1)], hop_send.at[5])
    whole(goes, note_send.at[0])
    whole(overs, note_send.at[1])
    for c in range(chunks):
        count = half - 1 if c < hopped else n - 1
        whole(pack.at[c, pl.ds(0, count)], kv_send.at[c])
        whole(pack.at[c, pl.ds(0, count)], kv_recv.at[c])
        own_copies[c].wait()
        if c < hopped:
            whole(far.at[c], far_send.at[c])

            @pl.when(is_gate)
            def _():
                for j in range(deep):
                    whole(pack.at[c, pl.ds(0, half - 1)], ward_send.at[c])
                whole(pack.at[c, pl.ds(0, (plane - 1) * deep)], ward_recv.at[c])

            @pl.when(jnp.logical_not(is_gate))
            def _():
                whole(pack.at[c, pl.ds(0, plane * deep)], ward_recv.at[c])


def kernel(n, plane, cap, hd, x_ref, wk_ref, wv_ref, len_in, own_in, pos_in, freq_in, q_in, gain_in, kg_in,
           att_ref, key_ref, val_ref,
           x, w, normed, kv, onehot, pack, flat, mine, q_all, part, stat, pa, sa, mid_p, mid_s, pb, sb, turn,
           len_ref, own_ref, pos_ref, freq_ref, q_ref, gain_ref, kg_ref,
           small_sem, x_sem, w_sem, own_sem, kv_send, kv_recv, hop_send, hop_recv):
    me = lax.axis_index("ctx")
    grp = lax.axis_index("groups")
    lines = n // plane
    line, spot = me // plane, me % plane
    rows, width = x.shape
    heads = mine.shape[0]
    kvh = wk_ref.shape[1] // hd
    group = heads // kvh
    chunk = w.shape[2]
    per = wk_ref.shape[1] // chunk
    chunks = 2 * per

    def loop(count, body):
        def step(i, carry):
            body(i)
            return carry
        lax.fori_loop(1, count, step, 0)

    def every(body):
        loop(n, lambda i: body(xor(me, n - i, n)))

    barrier = pltpu.get_barrier_semaphore()
    every(lambda d: pl.semaphore_signal(barrier, inc=1, device_id=(grp, d), device_id_type=MESH))

    smalls = {}
    for i, (name, src, dst) in enumerate((
        ("q", q_in, q_ref), ("own", own_in, own_ref), ("gain", gain_in, gain_ref), ("len", len_in, len_ref),
        ("pos", pos_in, pos_ref), ("freq", freq_in, freq_ref), ("kg", kg_in, kg_ref),
    )):
        smalls[name] = pltpu.make_async_copy(src, dst, small_sem.at[i])
        smalls[name].start()
    x_parts = x_sem.shape[0]
    xr = rows // x_parts
    x_copies = [
        pltpu.make_async_copy(x_ref.at[pl.ds(i * xr, xr)], x.at[pl.ds(i * xr, xr)], x_sem.at[i])
        for i in range(x_parts)
    ]
    for copy in x_copies:
        copy.start()
    w_copies = []
    for c in range(chunks):
        src = wv_ref if c < per else wk_ref
        copy = pltpu.make_async_copy(src.at[:, pl.ds((c % per) * chunk, chunk)], w.at[c], w_sem.at[c])
        w_copies.append(copy)
    w_copies[0].start()

    smalls["q"].wait()
    for h in range(heads):
        flat[h:h + 1, :] = q_ref[:, h * hd:(h + 1) * hd].astype(F32)
    mine[...] = flat[...].astype(BF16)

    smalls["own"].wait()
    own = own_ref[...]
    named = jnp.where(lax.broadcasted_iota(jnp.int32, (n, rows), 0) == own, 1.0, 0.0)
    earlier = jnp.where(
        lax.broadcasted_iota(jnp.int32, (rows, rows), 0) < lax.broadcasted_iota(jnp.int32, (rows, rows), 1), 1.0, 0.0
    ).astype(BF16)
    before = jnp.dot(named.astype(BF16), earlier, preferred_element_type=F32)
    rank = jnp.sum(before * named, axis=0, keepdims=True)
    slot = own.astype(F32) * cap + rank
    slots = n * cap
    step = 128
    for b in range(slots // step):
        places = (lax.broadcasted_iota(jnp.int32, (step, rows), 0) + b * step).astype(F32)
        onehot[pl.ds(b * step, step), :] = jnp.where(places == slot, 1.0, 0.0).astype(BF16)

    def send(src, dst, s_sem, r_sem, d):
        pltpu.make_async_remote_copy(
            src_ref=src, dst_ref=dst, send_sem=s_sem, recv_sem=r_sem, device_id=(grp, d), device_id_type=MESH
        ).start()

    def whole(ref, sem):
        pltpu.make_async_copy(ref, ref, sem).wait()

    def on_line(body):
        loop(lines, lambda i: body(xor(line, lines - i, lines)))

    def on_plane(body):
        loop(plane, lambda i: body(xor(spot, plane - i, plane)))

    smalls["gain"].wait()
    gain = gain_ref[...]
    tile = 16
    for i in range(x_parts):
        x_copies[i].wait()

        def norm(t, carry):
            at = pl.ds(pl.multiple_of(i * xr + t * tile, tile), tile)
            wide = x[at, :].astype(F32)
            scale = lax.rsqrt(jnp.mean(wide * wide, axis=-1, keepdims=True) + EPSILON)
            normed[at, :] = (wide * scale * gain).astype(BF16)
            return carry
        lax.fori_loop(0, xr // tile, norm, 0, unroll=True)
        if i == 0:
            for copy in w_copies[1:]:
                copy.start()

    own_copies = []

    def ship(c):
        out_ref = val_ref if c < per else key_ref
        cols = pl.ds((c % per) * chunk, chunk)
        packed = jnp.dot(onehot[...], kv[c], preferred_element_type=F32)
        pack[c] = packed.reshape(n, cap, chunk).astype(BF16)
        every(lambda d: send(pack.at[c, d], out_ref.at[me, :, cols], kv_send.at[c], kv_recv.at[c], d))
        copy = pltpu.make_async_copy(pack.at[c, me], out_ref.at[me, :, cols], own_sem.at[c])
        copy.start()
        own_copies.append(copy)

    def project(c):
        w_copies[c].wait()
        raw = jnp.dot(normed[...], w[c], preferred_element_type=F32)
        if c < per:
            kv[c] = raw.astype(BF16)
            return
        for h in range(chunk // hd):
            head = raw[:, h * hd:(h + 1) * hd]
            head = head * lax.rsqrt(jnp.mean(head * head, axis=-1, keepdims=True) + EPSILON) * kg_ref[...]
            turned = pltpu.roll(head, hd // 2, 1)
            kv[c, :, h * hd:(h + 1) * hd] = (head * turn[0] + turned * turn[1]).astype(BF16)

    project(0)
    pl.semaphore_wait(barrier, n - 1)
    on_line(lambda j: send(mine, q_all.at[line, spot], hop_send.at[0], hop_recv.at[0], j * plane + spot))
    q_all[line, spot] = mine[...]
    ship(0)
    for c in range(1, per):
        project(c)
        ship(c)
    whole(q_all.at[pl.ds(0, lines - 1), 0], hop_recv.at[0])
    on_plane(
        lambda j: send(q_all.at[:, spot], q_all.at[:, spot], hop_send.at[1], hop_recv.at[1], line * plane + j)
    )

    for name in ("len", "pos", "freq", "kg"):
        smalls[name].wait()
    angles = freq_ref[...] * pos_ref[...].astype(F32)
    cosine, sine = jnp.cos(angles), jnp.sin(angles)
    turn[0] = jnp.concatenate([cosine, cosine], axis=0).T
    turn[1] = jnp.concatenate([-sine, sine], axis=0).T
    for c in range(per, chunks):
        project(c)
        if c < chunks - 1:
            ship(c)

    row = me * rows + lax.broadcasted_iota(jnp.int32, (1, rows), 1)
    convs = len_ref.shape[0]
    row_conv, end = jnp.zeros((1, rows), jnp.int32), 0
    for j in range(convs):
        end = end + len_ref[j]
        row_conv = row_conv + jnp.where(row >= end, 1, 0)

    whole(q_all.at[:, pl.ds(0, plane - 1)], hop_recv.at[1])
    span = min(lines, max(1, 16 // plane))
    lined = span * plane * group
    per_conv = n // convs
    scale = 1.0 / (hd ** 0.5)
    in_chunk = chunk // hd

    def attend(b, carry):
        first = b * span * plane
        at = pl.ds(b * span, span)
        asks = (first + lax.broadcasted_iota(jnp.int32, (lined, rows), 0) // group) // per_conv
        allowed = asks == row_conv
        lane = lax.broadcasted_iota(jnp.int32, (lined, 128), 1)
        logs = jnp.zeros((lined, 128), F32)
        for k in range(kvh):
            q = q_all[at, :, k * group:(k + 1) * group, :].reshape(lined, hd)
            cols = slice((k % in_chunk) * hd, (k % in_chunk + 1) * hd)
            keys = kv[per + k // in_chunk, :, cols]
            values = kv[k // in_chunk, :, cols]
            scores = lax.dot_general(q, keys, (((1,), (1,)), ((), ())), preferred_element_type=F32) * scale
            scores = jnp.where(allowed, scores, MASKED)
            peak = jnp.max(scores, axis=-1, keepdims=True)
            expos = jnp.exp(scores - peak)
            sums = jnp.sum(expos, axis=-1, keepdims=True)
            mixed = jnp.dot(expos.astype(BF16), values, preferred_element_type=F32) / sums
            part[at, :, k * group:(k + 1) * group, :] = mixed.reshape(span, plane, group, hd).astype(BF16)
            logs = jnp.where(lane == k, peak + jnp.log(sums), logs)
        stat[at] = logs.reshape(span, plane, group, 128)
        return carry

    lax.fori_loop(0, lines // span, attend, 0)

    def give(j):
        send(part.at[:, j], pa.at[spot], hop_send.at[2], hop_recv.at[2], line * plane + j)
        send(stat.at[:, j], sa.at[spot], hop_send.at[3], hop_recv.at[3], line * plane + j)

    on_plane(give)
    pa[spot] = part[:, spot]
    sa[spot] = stat[:, spot]

    def merge(count, p_at, s_at):
        top = lax.fori_loop(0, count, lambda s, t: jnp.maximum(t, s_at(s)), jnp.full((group, 128), MASKED, F32))

        def add(s, carry):
            below, sums = carry
            factor = jnp.exp(s_at(s) - top)
            sums = tuple(sums[k] + factor[:, k:k + 1] * p_at(s, k).astype(F32) for k in range(kvh))
            return below + factor, sums

        zeros = jnp.zeros((group, 128), F32), tuple(jnp.zeros((group, hd), F32) for _ in range(kvh))
        below, sums = lax.fori_loop(0, count, add, zeros)
        return [(sums[k] / below[:, k:k + 1]).astype(BF16) for k in range(kvh)], top + jnp.log(below)

    whole(pa.at[pl.ds(0, plane - 1)], hop_recv.at[2])
    whole(sa.at[pl.ds(0, plane - 1)], hop_recv.at[3])

    def halfway(l, carry):
        mixed, logs = merge(
            plane, lambda s, k: pa[s, l, k * group:(k + 1) * group, :], lambda s: sa[s, l]
        )
        for k in range(kvh):
            mid_p[l, k * group:(k + 1) * group, :] = mixed[k]
        mid_s[l] = logs
        return carry

    lax.fori_loop(0, lines, halfway, 0)

    def give_on(j):
        send(mid_p.at[j], pb.at[line], hop_send.at[4], hop_recv.at[4], j * plane + spot)
        send(mid_s.at[j], sb.at[line], hop_send.at[5], hop_recv.at[5], j * plane + spot)

    on_line(give_on)
    pb[line] = mid_p[line]
    sb[line] = mid_s[line]
    ship(chunks - 1)
    whole(pb.at[pl.ds(0, lines - 1)], hop_recv.at[4])
    whole(sb.at[pl.ds(0, lines - 1)], hop_recv.at[5])
    mixed, _ = merge(lines, lambda s, k: pb[s, k * group:(k + 1) * group, :], lambda s: sb[s])
    for k in range(kvh):
        flat[k * group:(k + 1) * group, :] = mixed[k].astype(F32)
    for h in range(heads):
        att_ref[:, h * hd:(h + 1) * hd] = flat[h:h + 1, :].astype(BF16)

    whole(q_all.at[pl.ds(0, lines - 1), 0], hop_send.at[0])
    whole(q_all.at[:, pl.ds(0, plane - 1)], hop_send.at[1])
    whole(pa.at[pl.ds(0, plane - 1)], hop_send.at[2])
    whole(sa.at[pl.ds(0, plane - 1)], hop_send.at[3])
    whole(pb.at[pl.ds(0, lines - 1)], hop_send.at[4])
    whole(sb.at[pl.ds(0, lines - 1)], hop_send.at[5])
    for c in range(chunks):
        whole(pack.at[c, pl.ds(0, n - 1)], kv_send.at[c])
        whole(pack.at[c, pl.ds(0, n - 1)], kv_recv.at[c])
        own_copies[c].wait()


def on_device(hidden_rows, positions, owners, lengths, queries, ln_gain, w_key, w_value, k_gain):
    count, width = hidden_rows.shape
    n = lax.axis_size("ctx")
    grps = lax.axis_size("groups")
    hd = k_gain.shape[0]
    kv_width = w_key.shape[1]
    heads = queries.shape[1] // hd
    kvh = kv_width // hd
    group = heads // kvh
    cap = max(2, 2 * count // n)
    plane = 1
    while plane * plane < n:
        plane *= 2
    lines = n // plane
    half, deep = n // 2, lines // 2
    fill = 3 * count // 4
    freqs = np.float64(THETA) ** (-(np.arange(hd // 2) * 2.0) / hd)
    freqs = jnp.asarray(freqs.astype(np.float32)[:, None])

    chunk = 2 * hd
    chunks = 2 * kv_width // chunk
    hopped = chunks - 1
    vmem = pl.BlockSpec(memory_space=pltpu.VMEM)
    dma = pltpu.SemaphoreType.DMA
    caches = pltpu.VMEM((n, cap, kv_width), BF16)
    inputs = (
        hidden_rows, w_key, w_value, lengths, owners.reshape(1, count), positions.reshape(1, count), freqs, queries,
        ln_gain.reshape(1, width), k_gain.reshape(1, hd),
    )
    loaded = [
        pltpu.SMEM(lengths.shape, jnp.int32),
        pltpu.VMEM((1, count), jnp.int32),
        pltpu.VMEM((1, count), jnp.int32),
        pltpu.VMEM(freqs.shape, F32),
        pltpu.VMEM(queries.shape, BF16),
        pltpu.VMEM((1, width), F32),
        pltpu.VMEM((1, hd), F32),
    ]
    spread = [
        pltpu.VMEM((heads, hd), F32),
        pltpu.VMEM((heads, hd), BF16),
        pltpu.VMEM((lines, plane, heads, hd), BF16),
        pltpu.VMEM((lines, plane, heads, hd), BF16),
        pltpu.VMEM((lines, plane, group, 128), F32),
        pltpu.VMEM((plane, lines, heads, hd), BF16),
        pltpu.VMEM((plane, lines, group, 128), F32),
        pltpu.VMEM((lines, heads, hd), BF16),
        pltpu.VMEM((lines, group, 128), F32),
        pltpu.VMEM((lines, heads, hd), BF16),
        pltpu.VMEM((lines, group, 128), F32),
        pltpu.VMEM((2, count, hd), F32),
    ]
    big = [
        pltpu.VMEM((count, width), BF16),
        pltpu.VMEM((chunks, width, chunk), BF16),
        pltpu.VMEM((count, width), BF16),
        pltpu.VMEM((chunks, count, chunk), BF16),
        pltpu.VMEM((n * cap, count), BF16),
    ]
    pack = pltpu.VMEM((chunks, n, cap, chunk), BF16)
    sems = [dma((7,)), dma((4,)), dma((chunks,)), dma((chunks,)), dma((chunks,)), dma((chunks,)), dma((6,)), dma((6,))]

    attended, key_cache, value_cache, over = pl.pallas_call(
        functools.partial(fast_kernel, n, plane, cap, hd, fill),
        out_shape=(pltpu.VMEM((1, heads * hd), BF16), caches, caches, pltpu.SMEM((1,), F32)),
        in_specs=[pl.BlockSpec(memory_space=pltpu.HBM)] * 10,
        out_specs=(vmem, vmem, vmem, pl.BlockSpec(memory_space=pltpu.SMEM)),
        scratch_shapes=big + [
            pltpu.VMEM((fill, count), BF16),
            pack,
            pltpu.VMEM((hopped, fill, chunk), BF16),
            pltpu.VMEM((hopped, deep, fill, chunk), BF16),
            pltpu.VMEM((deep, half * cap, fill), BF16),
            pltpu.VMEM((hopped, deep, half, cap, chunk), BF16),
        ] + spread + [
            pltpu.VMEM((1, fill), F32),
            pltpu.VMEM((deep, 1, fill), F32),
            pltpu.VMEM((8, 128), F32),
            pltpu.VMEM((max(1, grps - 1), 8, 128), F32),
        ] + loaded + sems + [
            dma((hopped,)), dma((hopped,)), dma((hopped,)), dma((hopped,)), dma((2,)), dma((2,)),
        ],
        compiler_params=pltpu.CompilerParams(
            collective_id=0, has_side_effects=True, vmem_limit_bytes=60 * 1024 * 1024
        ),
        name="restore_attend",
    )(*inputs)

    def again(*_):
        return pl.pallas_call(
            functools.partial(kernel, n, plane, cap, hd),
            out_shape=(pltpu.VMEM((1, heads * hd), BF16), caches, caches),
            in_specs=[pl.BlockSpec(memory_space=pltpu.HBM)] * 10,
            out_specs=(vmem, vmem, vmem),
            scratch_shapes=big + [pack] + spread + loaded + sems,
            compiler_params=pltpu.CompilerParams(
                collective_id=1, has_side_effects=True, vmem_limit_bytes=60 * 1024 * 1024
            ),
            name="restore_attend_direct",
        )(*inputs)

    attended, key_cache, value_cache = lax.cond(
        over[0] > 0.5, again, lambda *done: done, attended, key_cache, value_cache
    )
    return attended, key_cache.reshape(n * cap, kv_width), value_cache.reshape(n * cap, kv_width)


def solution(mesh):
    rows = P(("groups", "ctx"), None)
    return jax.shard_map(
        on_device,
        mesh=mesh,
        in_specs=(rows, P(("groups", "ctx")), rows, P("groups"), rows, P(), P(), P(), P()),
        out_specs=(rows, rows, rows),
        check_vma=False,
    )
```

```python
import functools

import jax
import jax.numpy as jnp
import numpy as np
from jax import lax
from jax.experimental import pallas as pl
from jax.experimental.pallas import tpu as pltpu
from jax.sharding import PartitionSpec as P

EPSILON = 1e-06
THETA = 1000000.0
MASKED = -1e30
MESH = pl.DeviceIdType.MESH
F32 = jnp.float32
BF16 = jnp.bfloat16


def xor(a, b, n):
    out, bit = 0, 1
    while bit < n:
        p, q = (a // bit) % 2, (b // bit) % 2
        out = out + bit * (p + q - 2 * p * q)
        bit *= 2
    return out


def settle(a_in, k_in, v_in, a_out, k_out, v_out, sem):
    copies = [
        pltpu.make_async_copy(src, dst, sem.at[i])
        for i, (src, dst) in enumerate(((k_in, k_out), (v_in, v_out), (a_in, a_out)))
    ]
    for copy in copies:
        copy.start()
    for copy in copies:
        copy.wait()


def fast_kernel(n, plane, cap, hd, fill, x_ref, wk_ref, wv_ref, len_in, own_in, pos_in, freq_in, q_in, gain_in, kg_in,
                att_ref, key_ref, val_ref, over_ref,
                x, w, normed, kv, onehot, pick, pack, far, gate, place, ward, flat, mine, q_all, part, stat, pa, sa,
                mid_p, mid_s, pb, sb, turn, goes, comes, over, overs,
                len_ref, own_ref, pos_ref, freq_ref, q_ref, gain_ref, kg_ref,
                small_sem, x_sem, w_sem, own_sem, kv_send, kv_recv, hop_send, hop_recv,
                far_send, gate_recv, ward_send, ward_recv, note_send, note_recv):
    me = lax.axis_index("ctx")
    grp = lax.axis_index("groups")
    grps = lax.axis_size("groups")
    lines = n // plane
    line, spot = me // plane, me % plane
    half = n // 2
    deep = lines // 2
    side = me // half
    near = side * half
    gate_line = side * (deep - 1) + (1 - side) * deep
    my_gate = gate_line * plane + spot
    is_gate = line == (1 - side) * (deep - 1) + side * deep
    rows, width = x.shape
    heads = mine.shape[0]
    kvh = wk_ref.shape[1] // hd
    group = heads // kvh
    chunk = w.shape[2]
    per = wk_ref.shape[1] // chunk
    chunks = 2 * per
    hopped = gate.shape[0]

    def loop(count, body):
        def step(i, carry):
            body(i)
            return carry
        lax.fori_loop(1, count, step, 0)

    def every(body):
        loop(n, lambda i: body(xor(me, n - i, n)))

    def beside(body):
        loop(half, lambda i: body(xor(me, half - i, n)))

    def others(body):
        loop(grps, lambda i: body((grp + i) % grps, i - 1))

    barrier = pltpu.get_barrier_semaphore()
    every(lambda d: pl.semaphore_signal(barrier, inc=1, device_id=(grp, d), device_id_type=MESH))
    others(lambda g, i: pl.semaphore_signal(barrier, inc=1, device_id=(g, me), device_id_type=MESH))

    smalls = {}
    for i, (name, src, dst) in enumerate((
        ("q", q_in, q_ref), ("own", own_in, own_ref), ("gain", gain_in, gain_ref), ("len", len_in, len_ref),
        ("pos", pos_in, pos_ref), ("freq", freq_in, freq_ref), ("kg", kg_in, kg_ref),
    )):
        smalls[name] = pltpu.make_async_copy(src, dst, small_sem.at[i])
        smalls[name].start()
    x_parts = x_sem.shape[0]
    xr = rows // x_parts
    x_copies = [
        pltpu.make_async_copy(x_ref.at[pl.ds(i * xr, xr)], x.at[pl.ds(i * xr, xr)], x_sem.at[i])
        for i in range(x_parts)
    ]
    for copy in x_copies:
        copy.start()
    w_copies = []
    for c in range(chunks):
        src = wv_ref if c < per else wk_ref
        copy = pltpu.make_async_copy(src.at[:, pl.ds((c % per) * chunk, chunk)], w.at[c], w_sem.at[c])
        w_copies.append(copy)
    w_copies[0].start()

    smalls["q"].wait()
    for h in range(heads):
        flat[h:h + 1, :] = q_ref[:, h * hd:(h + 1) * hd].astype(F32)
    mine[...] = flat[...].astype(BF16)

    smalls["own"].wait()
    own = own_ref[...]
    named = jnp.where(lax.broadcasted_iota(jnp.int32, (n, rows), 0) == own, 1.0, 0.0)
    afar = jnp.where(own // half == side, 0.0, 1.0)
    marks = jnp.concatenate([named, jnp.broadcast_to(afar, (16, rows))], axis=0)
    earlier = jnp.where(
        lax.broadcasted_iota(jnp.int32, (rows, rows), 0) < lax.broadcasted_iota(jnp.int32, (rows, rows), 1), 1.0, 0.0
    ).astype(BF16)
    before = jnp.dot(marks.astype(BF16), earlier, preferred_element_type=F32)
    rank = jnp.sum(before[:n] * named, axis=0, keepdims=True)
    slot = own.astype(F32) * cap + rank
    slots = n * cap
    step = 128
    for b in range(slots // step):
        places = (lax.broadcasted_iota(jnp.int32, (step, rows), 0) + b * step).astype(F32)
        onehot[pl.ds(b * step, step), :] = jnp.where(places == slot, 1.0, 0.0).astype(BF16)
    seat = jnp.where(afar > 0.0, before[n:n + 1], -1.0)
    for b in range(fill // step):
        places = (lax.broadcasted_iota(jnp.int32, (step, rows), 0) + b * step).astype(F32)
        pick[pl.ds(b * step, step), :] = jnp.where(places == seat, 1.0, 0.0).astype(BF16)
    there = own.astype(F32) + 1.0
    facts = jnp.where(lax.broadcasted_iota(jnp.int32, (16, rows), 0) == 0, there, rank).astype(BF16)
    told = lax.dot_general(facts, pick[...], (((1,), (1,)), ((), ())), preferred_element_type=F32)
    goes[...] = (told[0:1] - 1.0 - ((1 - side) * half).astype(F32)) * cap + told[1:2]
    full = jnp.where(jnp.sum(afar, axis=1, keepdims=True) > fill, 1.0, 0.0)
    over[...] = jnp.broadcast_to(full, over.shape)

    def send(src, dst, s_sem, r_sem, d):
        pltpu.make_async_remote_copy(
            src_ref=src, dst_ref=dst, send_sem=s_sem, recv_sem=r_sem, device_id=(grp, d), device_id_type=MESH
        ).start()

    def tell(g, i):
        pltpu.make_async_remote_copy(
            src_ref=over, dst_ref=overs.at[i], send_sem=note_send.at[1], recv_sem=note_recv.at[1],
            device_id=(g, me), device_id_type=MESH
        ).start()

    def whole(ref, sem):
        pltpu.make_async_copy(ref, ref, sem).wait()

    def on_line(body):
        loop(lines, lambda i: body(xor(line, lines - i, lines)))

    def on_plane(body):
        loop(plane, lambda i: body(xor(spot, plane - i, plane)))

    smalls["gain"].wait()
    gain = gain_ref[...]
    tile = 16
    for i in range(x_parts):
        x_copies[i].wait()

        def norm(t, carry):
            at = pl.ds(pl.multiple_of(i * xr + t * tile, tile), tile)
            wide = x[at, :].astype(F32)
            scale = lax.rsqrt(jnp.mean(wide * wide, axis=-1, keepdims=True) + EPSILON)
            normed[at, :] = (wide * scale * gain).astype(BF16)
            return carry
        lax.fori_loop(0, xr // tile, norm, 0, unroll=True)
        if i == 0:
            for copy in w_copies[1:]:
                copy.start()

    own_copies = []

    def target(c):
        return val_ref if c < per else key_ref, pl.ds((c % per) * chunk, chunk)

    def keep(c):
        out_ref, cols = target(c)
        copy = pltpu.make_async_copy(pack.at[c, me], out_ref.at[me, :, cols], own_sem.at[c])
        copy.start()
        own_copies.append(copy)

    def hop(c):
        out_ref, cols = target(c)
        far[c] = jnp.dot(pick[...], kv[c], preferred_element_type=F32).astype(BF16)
        send(far.at[c], gate.at[c, line % deep], far_send.at[c], gate_recv.at[c], my_gate)
        at = pl.ds(pl.multiple_of(near * cap, half * cap), half * cap)
        packed = jnp.dot(onehot[at, :], kv[c], preferred_element_type=F32)
        pack[c, pl.ds(near, half)] = packed.reshape(half, cap, chunk).astype(BF16)
        beside(lambda d: send(pack.at[c, d], out_ref.at[me, :, cols], kv_send.at[c], kv_recv.at[c], d))
        keep(c)

    def ship(c):
        out_ref, cols = target(c)
        packed = jnp.dot(onehot[...], kv[c], preferred_element_type=F32)
        pack[c] = packed.reshape(n, cap, chunk).astype(BF16)
        beside(lambda d: send(pack.at[c, d], out_ref.at[me, :, cols], kv_send.at[c], kv_recv.at[c], d))
        keep(c)

    def cross(c):
        out_ref, cols = target(c)
        loop(half + 1, lambda i: send(
            pack.at[c, xor(me, n - i, n)], out_ref.at[me, :, cols], kv_send.at[c], kv_recv.at[c], xor(me, n - i, n)))

    def forward(c):
        out_ref, cols = target(c)

        @pl.when(is_gate)
        def _():
            whole(gate.at[c], gate_recv.at[c])
            if c == 0:
                whole(comes, note_recv.at[0])
                for j in range(deep):
                    for b in range(half * cap // step):
                        places = (lax.broadcasted_iota(jnp.int32, (step, fill), 0) + b * step).astype(F32)
                        place[j, pl.ds(b * step, step), :] = jnp.where(places == comes[j], 1.0, 0.0).astype(BF16)
            for j in range(deep):
                source = ((1 - side) * deep + j) * plane + spot
                spread = jnp.dot(place[j], gate[c, j], preferred_element_type=F32)
                ward[c, j] = spread.reshape(half, cap, chunk).astype(BF16)
                beside(lambda d: send(
                    ward.at[c, j, d - near], out_ref.at[source, :, cols], ward_send.at[c], ward_recv.at[c], d))
                out_ref[source, :, cols] = ward[c, j, me - near]

    def project(c):
        w_copies[c].wait()
        raw = jnp.dot(normed[...], w[c], preferred_element_type=F32)
        if c < per:
            kv[c] = raw.astype(BF16)
            return
        for h in range(chunk // hd):
            head = raw[:, h * hd:(h + 1) * hd]
            head = head * lax.rsqrt(jnp.mean(head * head, axis=-1, keepdims=True) + EPSILON) * kg_ref[...]
            turned = pltpu.roll(head, hd // 2, 1)
            kv[c, :, h * hd:(h + 1) * hd] = (head * turn[0] + turned * turn[1]).astype(BF16)

    project(0)
    pl.semaphore_wait(barrier, n - 1 + grps - 1)
    on_line(lambda j: send(mine, q_all.at[line, spot], hop_send.at[0], hop_recv.at[0], j * plane + spot))
    send(goes, comes.at[line % deep], note_send.at[0], note_recv.at[0], my_gate)
    others(tell)
    q_all[line, spot] = mine[...]
    hop(0)
    for c in range(1, per):
        project(c)
        hop(c)
    whole(q_all.at[pl.ds(0, lines - 1), 0], hop_recv.at[0])
    on_plane(
        lambda j: send(q_all.at[:, spot], q_all.at[:, spot], hop_send.at[1], hop_recv.at[1], line * plane + j)
    )

    for name in ("len", "pos", "freq", "kg"):
        smalls[name].wait()
    angles = freq_ref[...] * pos_ref[...].astype(F32)
    cosine, sine = jnp.cos(angles), jnp.sin(angles)
    turn[0] = jnp.concatenate([cosine, cosine], axis=0).T
    turn[1] = jnp.concatenate([-sine, sine], axis=0).T
    for c in range(per, chunks):
        project(c)
        hop(c) if c < hopped else ship(c)

    row = me * rows + lax.broadcasted_iota(jnp.int32, (1, rows), 1)
    convs = len_ref.shape[0]
    row_conv, end = jnp.zeros((1, rows), jnp.int32), 0
    for j in range(convs):
        end = end + len_ref[j]
        row_conv = row_conv + jnp.where(row >= end, 1, 0)

    whole(overs, note_recv.at[1])
    flag = over[0:1, :]
    for i in range(overs.shape[0]):
        flag = jnp.maximum(flag, overs[i, 0:1, :])

    whole(q_all.at[:, pl.ds(0, plane - 1)], hop_recv.at[1])
    span = min(lines, max(1, 16 // plane))
    lined = span * plane * group
    per_conv = n // convs
    scale = 1.0 / (hd ** 0.5)
    in_chunk = chunk // hd

    def attend(b, carry):
        first = b * span * plane
        at = pl.ds(b * span, span)
        asks = (first + lax.broadcasted_iota(jnp.int32, (lined, rows), 0) // group) // per_conv
        allowed = asks == row_conv
        lane = lax.broadcasted_iota(jnp.int32, (lined, 128), 1)
        logs = jnp.where(lane == 127, flag, 0.0)
        for k in range(kvh):
            q = q_all[at, :, k * group:(k + 1) * group, :].reshape(lined, hd)
            cols = slice((k % in_chunk) * hd, (k % in_chunk + 1) * hd)
            keys = kv[per + k // in_chunk, :, cols]
            values = kv[k // in_chunk, :, cols]
            scores = lax.dot_general(q, keys, (((1,), (1,)), ((), ())), preferred_element_type=F32) * scale
            scores = jnp.where(allowed, scores, MASKED)
            peak = jnp.max(scores, axis=-1, keepdims=True)
            expos = jnp.exp(scores - peak)
            sums = jnp.sum(expos, axis=-1, keepdims=True)
            mixed = jnp.dot(expos.astype(BF16), values, preferred_element_type=F32) / sums
            part[at, :, k * group:(k + 1) * group, :] = mixed.reshape(span, plane, group, hd).astype(BF16)
            logs = jnp.where(lane == k, peak + jnp.log(sums), logs)
        stat[at] = logs.reshape(span, plane, group, 128)
        return carry

    lax.fori_loop(0, lines // span, attend, 0)

    def give(j):
        send(part.at[:, j], pa.at[spot], hop_send.at[2], hop_recv.at[2], line * plane + j)
        send(stat.at[:, j], sa.at[spot], hop_send.at[3], hop_recv.at[3], line * plane + j)

    on_plane(give)
    pa[spot] = part[:, spot]
    sa[spot] = stat[:, spot]
    forward(0)
    forward(1)

    def merge(count, p_at, s_at):
        top = lax.fori_loop(0, count, lambda s, t: jnp.maximum(t, s_at(s)), jnp.full((group, 128), MASKED, F32))

        def add(s, carry):
            below, sums = carry
            factor = jnp.exp(s_at(s) - top)
            sums = tuple(sums[k] + factor[:, k:k + 1] * p_at(s, k).astype(F32) for k in range(kvh))
            return below + factor, sums

        zeros = jnp.zeros((group, 128), F32), tuple(jnp.zeros((group, hd), F32) for _ in range(kvh))
        below, sums = lax.fori_loop(0, count, add, zeros)
        lane = lax.broadcasted_iota(jnp.int32, (group, 128), 1)
        logs = jnp.where(lane == 127, top, top + jnp.log(below))
        return [(sums[k] / below[:, k:k + 1]).astype(BF16) for k in range(kvh)], logs

    whole(pa.at[pl.ds(0, plane - 1)], hop_recv.at[2])
    whole(sa.at[pl.ds(0, plane - 1)], hop_recv.at[3])

    def halfway(l, carry):
        mixed, logs = merge(
            plane, lambda s, k: pa[s, l, k * group:(k + 1) * group, :], lambda s: sa[s, l]
        )
        for k in range(kvh):
            mid_p[l, k * group:(k + 1) * group, :] = mixed[k]
        mid_s[l] = logs
        return carry

    lax.fori_loop(0, lines, halfway, 0)

    def give_on(j):
        send(mid_p.at[j], pb.at[line], hop_send.at[4], hop_recv.at[4], j * plane + spot)
        send(mid_s.at[j], sb.at[line], hop_send.at[5], hop_recv.at[5], j * plane + spot)

    on_line(give_on)
    pb[line] = mid_p[line]
    sb[line] = mid_s[line]
    for c in range(hopped, chunks):
        cross(c)
    for c in range(2, hopped):
        forward(c)
    whole(pb.at[pl.ds(0, lines - 1)], hop_recv.at[4])
    whole(sb.at[pl.ds(0, lines - 1)], hop_recv.at[5])
    mixed, logs = merge(lines, lambda s, k: pb[s, k * group:(k + 1) * group, :], lambda s: sb[s])
    lane = lax.broadcasted_iota(jnp.int32, (group, 128), 1)
    over_ref[0] = jnp.max(jnp.where(lane == 127, logs, 0.0))
    for k in range(kvh):
        flat[k * group:(k + 1) * group, :] = mixed[k].astype(F32)
    for h in range(heads):
        att_ref[:, h * hd:(h + 1) * hd] = flat[h:h + 1, :].astype(BF16)

    whole(q_all.at[pl.ds(0, lines - 1), 0], hop_send.at[0])
    whole(q_all.at[:, pl.ds(0, plane - 1)], hop_send.at[1])
    whole(pa.at[pl.ds(0, plane - 1)], hop_send.at[2])
    whole(sa.at[pl.ds(0, plane - 1)], hop_send.at[3])
    whole(pb.at[pl.ds(0, lines - 1)], hop_send.at[4])
    whole(sb.at[pl.ds(0, lines - 1)], hop_send.at[5])
    whole(goes, note_send.at[0])
    whole(overs, note_send.at[1])
    for c in range(chunks):
        count = half - 1 if c < hopped else n - 1
        whole(pack.at[c, pl.ds(0, count)], kv_send.at[c])
        whole(pack.at[c, pl.ds(0, count)], kv_recv.at[c])
        own_copies[c].wait()
        if c < hopped:
            whole(far.at[c], far_send.at[c])

            @pl.when(is_gate)
            def _():
                for j in range(deep):
                    whole(pack.at[c, pl.ds(0, half - 1)], ward_send.at[c])
                whole(pack.at[c, pl.ds(0, (plane - 1) * deep)], ward_recv.at[c])

            @pl.when(jnp.logical_not(is_gate))
            def _():
                whole(pack.at[c, pl.ds(0, plane * deep)], ward_recv.at[c])


def kernel(n, plane, cap, hd, x_ref, wk_ref, wv_ref, len_in, own_in, pos_in, freq_in, q_in, gain_in, kg_in,
           att_ref, key_ref, val_ref,
           x, w, normed, kv, onehot, pack, flat, mine, q_all, part, stat, pa, sa, mid_p, mid_s, pb, sb, turn,
           len_ref, own_ref, pos_ref, freq_ref, q_ref, gain_ref, kg_ref,
           small_sem, x_sem, w_sem, own_sem, kv_send, kv_recv, hop_send, hop_recv):
    me = lax.axis_index("ctx")
    grp = lax.axis_index("groups")
    lines = n // plane
    line, spot = me // plane, me % plane
    rows, width = x.shape
    heads = mine.shape[0]
    kvh = wk_ref.shape[1] // hd
    group = heads // kvh
    chunk = w.shape[2]
    per = wk_ref.shape[1] // chunk
    chunks = 2 * per

    def loop(count, body):
        def step(i, carry):
            body(i)
            return carry
        lax.fori_loop(1, count, step, 0)

    def every(body):
        loop(n, lambda i: body(xor(me, n - i, n)))

    barrier = pltpu.get_barrier_semaphore()
    every(lambda d: pl.semaphore_signal(barrier, inc=1, device_id=(grp, d), device_id_type=MESH))

    smalls = {}
    for i, (name, src, dst) in enumerate((
        ("q", q_in, q_ref), ("own", own_in, own_ref), ("gain", gain_in, gain_ref), ("len", len_in, len_ref),
        ("pos", pos_in, pos_ref), ("freq", freq_in, freq_ref), ("kg", kg_in, kg_ref),
    )):
        smalls[name] = pltpu.make_async_copy(src, dst, small_sem.at[i])
        smalls[name].start()
    x_parts = x_sem.shape[0]
    xr = rows // x_parts
    x_copies = [
        pltpu.make_async_copy(x_ref.at[pl.ds(i * xr, xr)], x.at[pl.ds(i * xr, xr)], x_sem.at[i])
        for i in range(x_parts)
    ]
    for copy in x_copies:
        copy.start()
    w_copies = []
    for c in range(chunks):
        src = wv_ref if c < per else wk_ref
        copy = pltpu.make_async_copy(src.at[:, pl.ds((c % per) * chunk, chunk)], w.at[c], w_sem.at[c])
        w_copies.append(copy)
    w_copies[0].start()

    smalls["q"].wait()
    for h in range(heads):
        flat[h:h + 1, :] = q_ref[:, h * hd:(h + 1) * hd].astype(F32)
    mine[...] = flat[...].astype(BF16)

    smalls["own"].wait()
    own = own_ref[...]
    named = jnp.where(lax.broadcasted_iota(jnp.int32, (n, rows), 0) == own, 1.0, 0.0)
    earlier = jnp.where(
        lax.broadcasted_iota(jnp.int32, (rows, rows), 0) < lax.broadcasted_iota(jnp.int32, (rows, rows), 1), 1.0, 0.0
    ).astype(BF16)
    before = jnp.dot(named.astype(BF16), earlier, preferred_element_type=F32)
    rank = jnp.sum(before * named, axis=0, keepdims=True)
    slot = own.astype(F32) * cap + rank
    slots = n * cap
    step = 128
    for b in range(slots // step):
        places = (lax.broadcasted_iota(jnp.int32, (step, rows), 0) + b * step).astype(F32)
        onehot[pl.ds(b * step, step), :] = jnp.where(places == slot, 1.0, 0.0).astype(BF16)

    def send(src, dst, s_sem, r_sem, d):
        pltpu.make_async_remote_copy(
            src_ref=src, dst_ref=dst, send_sem=s_sem, recv_sem=r_sem, device_id=(grp, d), device_id_type=MESH
        ).start()

    def whole(ref, sem):
        pltpu.make_async_copy(ref, ref, sem).wait()

    def on_line(body):
        loop(lines, lambda i: body(xor(line, lines - i, lines)))

    def on_plane(body):
        loop(plane, lambda i: body(xor(spot, plane - i, plane)))

    smalls["gain"].wait()
    gain = gain_ref[...]
    tile = 16
    for i in range(x_parts):
        x_copies[i].wait()

        def norm(t, carry):
            at = pl.ds(pl.multiple_of(i * xr + t * tile, tile), tile)
            wide = x[at, :].astype(F32)
            scale = lax.rsqrt(jnp.mean(wide * wide, axis=-1, keepdims=True) + EPSILON)
            normed[at, :] = (wide * scale * gain).astype(BF16)
            return carry
        lax.fori_loop(0, xr // tile, norm, 0, unroll=True)
        if i == 0:
            for copy in w_copies[1:]:
                copy.start()

    own_copies = []

    def ship(c):
        out_ref = val_ref if c < per else key_ref
        cols = pl.ds((c % per) * chunk, chunk)
        packed = jnp.dot(onehot[...], kv[c], preferred_element_type=F32)
        pack[c] = packed.reshape(n, cap, chunk).astype(BF16)
        every(lambda d: send(pack.at[c, d], out_ref.at[me, :, cols], kv_send.at[c], kv_recv.at[c], d))
        copy = pltpu.make_async_copy(pack.at[c, me], out_ref.at[me, :, cols], own_sem.at[c])
        copy.start()
        own_copies.append(copy)

    def project(c):
        w_copies[c].wait()
        raw = jnp.dot(normed[...], w[c], preferred_element_type=F32)
        if c < per:
            kv[c] = raw.astype(BF16)
            return
        for h in range(chunk // hd):
            head = raw[:, h * hd:(h + 1) * hd]
            head = head * lax.rsqrt(jnp.mean(head * head, axis=-1, keepdims=True) + EPSILON) * kg_ref[...]
            turned = pltpu.roll(head, hd // 2, 1)
            kv[c, :, h * hd:(h + 1) * hd] = (head * turn[0] + turned * turn[1]).astype(BF16)

    project(0)
    pl.semaphore_wait(barrier, n - 1)
    on_line(lambda j: send(mine, q_all.at[line, spot], hop_send.at[0], hop_recv.at[0], j * plane + spot))
    q_all[line, spot] = mine[...]
    ship(0)
    for c in range(1, per):
        project(c)
        ship(c)
    whole(q_all.at[pl.ds(0, lines - 1), 0], hop_recv.at[0])
    on_plane(
        lambda j: send(q_all.at[:, spot], q_all.at[:, spot], hop_send.at[1], hop_recv.at[1], line * plane + j)
    )

    for name in ("len", "pos", "freq", "kg"):
        smalls[name].wait()
    angles = freq_ref[...] * pos_ref[...].astype(F32)
    cosine, sine = jnp.cos(angles), jnp.sin(angles)
    turn[0] = jnp.concatenate([cosine, cosine], axis=0).T
    turn[1] = jnp.concatenate([-sine, sine], axis=0).T
    for c in range(per, chunks):
        project(c)
        if c < chunks - 1:
            ship(c)

    row = me * rows + lax.broadcasted_iota(jnp.int32, (1, rows), 1)
    convs = len_ref.shape[0]
    row_conv, end = jnp.zeros((1, rows), jnp.int32), 0
    for j in range(convs):
        end = end + len_ref[j]
        row_conv = row_conv + jnp.where(row >= end, 1, 0)

    whole(q_all.at[:, pl.ds(0, plane - 1)], hop_recv.at[1])
    span = min(lines, max(1, 16 // plane))
    lined = span * plane * group
    per_conv = n // convs
    scale = 1.0 / (hd ** 0.5)
    in_chunk = chunk // hd

    def attend(b, carry):
        first = b * span * plane
        at = pl.ds(b * span, span)
        asks = (first + lax.broadcasted_iota(jnp.int32, (lined, rows), 0) // group) // per_conv
        allowed = asks == row_conv
        lane = lax.broadcasted_iota(jnp.int32, (lined, 128), 1)
        logs = jnp.zeros((lined, 128), F32)
        for k in range(kvh):
            q = q_all[at, :, k * group:(k + 1) * group, :].reshape(lined, hd)
            cols = slice((k % in_chunk) * hd, (k % in_chunk + 1) * hd)
            keys = kv[per + k // in_chunk, :, cols]
            values = kv[k // in_chunk, :, cols]
            scores = lax.dot_general(q, keys, (((1,), (1,)), ((), ())), preferred_element_type=F32) * scale
            scores = jnp.where(allowed, scores, MASKED)
            peak = jnp.max(scores, axis=-1, keepdims=True)
            expos = jnp.exp(scores - peak)
            sums = jnp.sum(expos, axis=-1, keepdims=True)
            mixed = jnp.dot(expos.astype(BF16), values, preferred_element_type=F32) / sums
            part[at, :, k * group:(k + 1) * group, :] = mixed.reshape(span, plane, group, hd).astype(BF16)
            logs = jnp.where(lane == k, peak + jnp.log(sums), logs)
        stat[at] = logs.reshape(span, plane, group, 128)
        return carry

    lax.fori_loop(0, lines // span, attend, 0)

    def give(j):
        send(part.at[:, j], pa.at[spot], hop_send.at[2], hop_recv.at[2], line * plane + j)
        send(stat.at[:, j], sa.at[spot], hop_send.at[3], hop_recv.at[3], line * plane + j)

    on_plane(give)
    pa[spot] = part[:, spot]
    sa[spot] = stat[:, spot]

    def merge(count, p_at, s_at):
        top = lax.fori_loop(0, count, lambda s, t: jnp.maximum(t, s_at(s)), jnp.full((group, 128), MASKED, F32))

        def add(s, carry):
            below, sums = carry
            factor = jnp.exp(s_at(s) - top)
            sums = tuple(sums[k] + factor[:, k:k + 1] * p_at(s, k).astype(F32) for k in range(kvh))
            return below + factor, sums

        zeros = jnp.zeros((group, 128), F32), tuple(jnp.zeros((group, hd), F32) for _ in range(kvh))
        below, sums = lax.fori_loop(0, count, add, zeros)
        return [(sums[k] / below[:, k:k + 1]).astype(BF16) for k in range(kvh)], top + jnp.log(below)

    whole(pa.at[pl.ds(0, plane - 1)], hop_recv.at[2])
    whole(sa.at[pl.ds(0, plane - 1)], hop_recv.at[3])

    def halfway(l, carry):
        mixed, logs = merge(
            plane, lambda s, k: pa[s, l, k * group:(k + 1) * group, :], lambda s: sa[s, l]
        )
        for k in range(kvh):
            mid_p[l, k * group:(k + 1) * group, :] = mixed[k]
        mid_s[l] = logs
        return carry

    lax.fori_loop(0, lines, halfway, 0)

    def give_on(j):
        send(mid_p.at[j], pb.at[line], hop_send.at[4], hop_recv.at[4], j * plane + spot)
        send(mid_s.at[j], sb.at[line], hop_send.at[5], hop_recv.at[5], j * plane + spot)

    on_line(give_on)
    pb[line] = mid_p[line]
    sb[line] = mid_s[line]
    ship(chunks - 1)
    whole(pb.at[pl.ds(0, lines - 1)], hop_recv.at[4])
    whole(sb.at[pl.ds(0, lines - 1)], hop_recv.at[5])
    mixed, _ = merge(lines, lambda s, k: pb[s, k * group:(k + 1) * group, :], lambda s: sb[s])
    for k in range(kvh):
        flat[k * group:(k + 1) * group, :] = mixed[k].astype(F32)
    for h in range(heads):
        att_ref[:, h * hd:(h + 1) * hd] = flat[h:h + 1, :].astype(BF16)

    whole(q_all.at[pl.ds(0, lines - 1), 0], hop_send.at[0])
    whole(q_all.at[:, pl.ds(0, plane - 1)], hop_send.at[1])
    whole(pa.at[pl.ds(0, plane - 1)], hop_send.at[2])
    whole(sa.at[pl.ds(0, plane - 1)], hop_send.at[3])
    whole(pb.at[pl.ds(0, lines - 1)], hop_send.at[4])
    whole(sb.at[pl.ds(0, lines - 1)], hop_send.at[5])
    for c in range(chunks):
        whole(pack.at[c, pl.ds(0, n - 1)], kv_send.at[c])
        whole(pack.at[c, pl.ds(0, n - 1)], kv_recv.at[c])
        own_copies[c].wait()


def on_device(hidden_rows, positions, owners, lengths, queries, ln_gain, w_key, w_value, k_gain):
    count, width = hidden_rows.shape
    n = lax.axis_size("ctx")
    grps = lax.axis_size("groups")
    hd = k_gain.shape[0]
    kv_width = w_key.shape[1]
    heads = queries.shape[1] // hd
    kvh = kv_width // hd
    group = heads // kvh
    cap = max(2, 2 * count // n)
    plane = 1
    while plane * plane < n:
        plane *= 2
    lines = n // plane
    half, deep = n // 2, lines // 2
    fill = 3 * count // 4
    freqs = np.float64(THETA) ** (-(np.arange(hd // 2) * 2.0) / hd)
    freqs = jnp.asarray(freqs.astype(np.float32)[:, None])

    chunk = 2 * hd
    chunks = 2 * kv_width // chunk
    hopped = chunks - 1
    vmem = pl.BlockSpec(memory_space=pltpu.VMEM)
    dma = pltpu.SemaphoreType.DMA
    caches = pltpu.VMEM((n, cap, kv_width), BF16)
    inputs = (
        hidden_rows, w_key, w_value, lengths, owners.reshape(1, count), positions.reshape(1, count), freqs, queries,
        ln_gain.reshape(1, width), k_gain.reshape(1, hd),
    )
    loaded = [
        pltpu.SMEM(lengths.shape, jnp.int32),
        pltpu.VMEM((1, count), jnp.int32),
        pltpu.VMEM((1, count), jnp.int32),
        pltpu.VMEM(freqs.shape, F32),
        pltpu.VMEM(queries.shape, BF16),
        pltpu.VMEM((1, width), F32),
        pltpu.VMEM((1, hd), F32),
    ]
    spread = [
        pltpu.VMEM((heads, hd), F32),
        pltpu.VMEM((heads, hd), BF16),
        pltpu.VMEM((lines, plane, heads, hd), BF16),
        pltpu.VMEM((lines, plane, heads, hd), BF16),
        pltpu.VMEM((lines, plane, group, 128), F32),
        pltpu.VMEM((plane, lines, heads, hd), BF16),
        pltpu.VMEM((plane, lines, group, 128), F32),
        pltpu.VMEM((lines, heads, hd), BF16),
        pltpu.VMEM((lines, group, 128), F32),
        pltpu.VMEM((lines, heads, hd), BF16),
        pltpu.VMEM((lines, group, 128), F32),
        pltpu.VMEM((2, count, hd), F32),
    ]
    big = [
        pltpu.VMEM((count, width), BF16),
        pltpu.VMEM((chunks, width, chunk), BF16),
        pltpu.VMEM((count, width), BF16),
        pltpu.VMEM((chunks, count, chunk), BF16),
        pltpu.VMEM((n * cap, count), BF16),
    ]
    pack = pltpu.VMEM((chunks, n, cap, chunk), BF16)
    sems = [dma((7,)), dma((4,)), dma((chunks,)), dma((chunks,)), dma((chunks,)), dma((chunks,)), dma((6,)), dma((6,))]

    attended, key_cache, value_cache, over = pl.pallas_call(
        functools.partial(fast_kernel, n, plane, cap, hd, fill),
        out_shape=(pltpu.VMEM((1, heads * hd), BF16), caches, caches, pltpu.SMEM((1,), F32)),
        in_specs=[pl.BlockSpec(memory_space=pltpu.HBM)] * 10,
        out_specs=(vmem, vmem, vmem, pl.BlockSpec(memory_space=pltpu.SMEM)),
        scratch_shapes=big + [
            pltpu.VMEM((fill, count), BF16),
            pack,
            pltpu.VMEM((hopped, fill, chunk), BF16),
            pltpu.VMEM((hopped, deep, fill, chunk), BF16),
            pltpu.VMEM((deep, half * cap, fill), BF16),
            pltpu.VMEM((hopped, deep, half, cap, chunk), BF16),
        ] + spread + [
            pltpu.VMEM((1, fill), F32),
            pltpu.VMEM((deep, 1, fill), F32),
            pltpu.VMEM((8, 128), F32),
            pltpu.VMEM((max(1, grps - 1), 8, 128), F32),
        ] + loaded + sems + [
            dma((hopped,)), dma((hopped,)), dma((hopped,)), dma((hopped,)), dma((2,)), dma((2,)),
        ],
        compiler_params=pltpu.CompilerParams(
            collective_id=0, has_side_effects=True, vmem_limit_bytes=60 * 1024 * 1024
        ),
        name="restore_attend",
    )(*inputs)

    def again(*_):
        return pl.pallas_call(
            functools.partial(kernel, n, plane, cap, hd),
            out_shape=(pltpu.VMEM((1, heads * hd), BF16), caches, caches),
            in_specs=[pl.BlockSpec(memory_space=pltpu.HBM)] * 10,
            out_specs=(vmem, vmem, vmem),
            scratch_shapes=big + [pack] + spread + loaded + sems,
            compiler_params=pltpu.CompilerParams(
                collective_id=1, has_side_effects=True, vmem_limit_bytes=60 * 1024 * 1024
            ),
            name="restore_attend_direct",
        )(*inputs)

    attended, key_cache, value_cache = lax.cond(
        over[0] > 0.5, again, lambda *done: done, attended, key_cache, value_cache
    )
    hbm = pl.BlockSpec(memory_space=pltpu.HBM)
    attended, key_cache, value_cache = pl.pallas_call(
        settle,
        out_shape=(
            jax.ShapeDtypeStruct((1, heads * hd), BF16),
            jax.ShapeDtypeStruct((n, cap, kv_width), BF16),
            jax.ShapeDtypeStruct((n, cap, kv_width), BF16),
        ),
        in_specs=[vmem] * 3,
        out_specs=(hbm, hbm, hbm),
        scratch_shapes=[dma((3,))],
        name="settle",
    )(attended, key_cache, value_cache)
    return attended, key_cache.reshape(n * cap, kv_width), value_cache.reshape(n * cap, kv_width)


def solution(mesh):
    rows = P(("groups", "ctx"), None)
    return jax.shard_map(
        on_device,
        mesh=mesh,
        in_specs=(rows, P(("groups", "ctx")), rows, P("groups"), rows, P(), P(), P(), P()),
        out_specs=(rows, rows, rows),
        check_vma=False,
    )
```
